512 devices in a mesh: facet: 64 (over y_hi, z, x), band: 8 (over y_lo, core).
Axes of the slice: x: 4, y: 8 (y_hi: 2, y_lo: 4; y = y_hi * 4 + y_lo), z: 8, core: 2. Of those that a mesh axis runs over, the one named last changes fastest.
Arguments:
- facet_strips: float32 [8, 64, 2, 8, 4096], P('band', 'facet'), may hold values from -6 to 6
- subgrid_offsets: int32 [2, 64], replicated, may hold values from 0 to 4095
- sample_cells: int32 [8, 2, 64, 2, 512], P('band', None, 'facet'), may hold values from 0 to 511, as said below
- sample_values: float32 [8, 2, 64, 2, 512], P('band', None, 'facet'), may hold values from -6 to 6
- sample_weights: float32 [8, 2, 64, 512], P('band', None, 'facet'), may hold values from 0.1 to 1
- sample_flags: int32 [8, 2, 64, 512], P('band', None, 'facet'), may hold values 0 or 1
Outputs:
- residual_strips: float32 [64, 8, 2, 4096], P('facet', 'band')
The draws below stay inside these ranges and needn't reach their ends.
Inputs may be any that keep to these rules, and one draw needn't show every extreme that they name: `sample_cells`: slot 0 holds a row of 0 to (64 // 8) * 8 - 1, slot 1 a column of 0 to 512 - 1; every subgrid of every sub-band and front has a sample at its last row and last column.
All inputs are finite; a program needn't handle non-finite values. No bound on the sum of `sample_flags` on one device may be relied on, other than what follows from the above.
Results may differ from the reference program's by a relative error of at most 0.006.
Values may be sent and summed in bfloat16 or wider, within the bound.
A program may use at most 64 MiB of HBM per device.

```python
import math
import jax
import jax.numpy as jnp
from jax import lax

FN = 4096
CONTRIB = 64
FACET_ROWS = 8
COLS = 8
FRONTS = 2
VIS = 512
FACETS = 64
BANDS = 8
SG = 512
CELLS = 32768


def draw_sample_cells(key, part):
    row_total = FACETS // FACET_ROWS * COLS
    key_row = jax.random.fold_in(key, 11)
    key_col = jax.random.fold_in(key, 23)
    row_draw = jax.random.randint(key_row, (BANDS, FRONTS, FACETS, 1, VIS), 0, row_total, dtype=jnp.int32)
    col_draw = jax.random.randint(key_col, (BANDS, FRONTS, FACETS, 1, VIS), 0, SG, dtype=jnp.int32)
    row_draw = row_draw.at[..., 0].set(row_total - 1).at[..., 1].set(0)
    col_draw = col_draw.at[..., 0].set(SG - 1).at[..., 1].set(0)
    return jnp.concatenate([row_draw, col_draw], axis=3).astype(jnp.int32)


def place_ends(result, stream_key, least, high):
    spot = [jax.random.randint(jax.random.fold_in(stream_key, axis), (), 0, length) for axis, length in enumerate(result.shape)]
    widest = result.shape.index(max(result.shape))
    beside = spot[:widest] + [(spot[widest] + 1) % result.shape[widest]] + spot[widest + 1:]
    return result.at[tuple(spot)].set(least).at[tuple(beside)].set(high)


def shard_levels(own_key, extent, shards, low, top_value):
    loudness, own = 1.0, jax.random.fold_in(own_key, 6)
    for position, blocks in shards:
        steps = jnp.exp(jax.random.uniform(jax.random.fold_in(own, position), (blocks,), jnp.float32, low / len(shards), top_value / len(shards)))
        loudness = loudness * jnp.repeat(steps, extent[position] // blocks).reshape([-1 if axis == position else 1 for axis in range(len(extent))])
    return loudness


def noise(key, shape, deviation, most, cuts=(), held_as=jnp.bfloat16):
    level = shard_levels(key, shape, cuts, -0.22, 0.18) if cuts else 1.0
    array = jax.random.normal(key, shape, jnp.float32) * deviation * level
    return jnp.minimum(jnp.maximum(array, -most), most).astype(held_as)


def setup_inputs(seed: int = 0) -> dict:
    splits = jax.random.split(jax.random.key(seed), 7)
    facet_strips = noise(splits[0], (BANDS, FACETS, 2, COLS, FN), 1.0, 6.0, ((0, 8), (1, 64)), jnp.float32)
    subgrid_offsets = place_ends(jax.random.randint(splits[1], (FRONTS, FACETS), 0, FN), jax.random.fold_in(splits[1], 1), 0, FN - 1).astype(jnp.int32)
    sample_cells = draw_sample_cells(jax.random.fold_in(splits[6], 71), 0)
    sample_values = noise(splits[3], (BANDS, FRONTS, FACETS, 2, VIS), 1.0, 6.0, ((0, 8), (2, 64)), jnp.float32)
    sample_weights = jnp.clip(jnp.exp(math.log(1.0) - 2.3025851 * jax.random.uniform(splits[4], (BANDS, FRONTS, FACETS, VIS), jnp.float32) ** shard_levels(splits[4], (BANDS, FRONTS, FACETS, VIS), ((0, 8), (2, 64)), -0.2, 0.2)), 0.1, 1.0)
    sample_flags = place_ends((jax.random.randint(splits[5], (BANDS, FRONTS, FACETS, VIS), 0, 8) < 7).astype(jnp.int32), jax.random.fold_in(splits[5], 1), 0, 1)
    return {"facet_strips": facet_strips, "subgrid_offsets": subgrid_offsets, "sample_cells": sample_cells, "sample_values": sample_values, "sample_weights": sample_weights, "sample_flags": sample_flags}


def to_complex(real_part, imag_part):
    return lax.complex(real_part, imag_part)


def rounded(values):
    real_part = lax.optimization_barrier(jnp.real(values).astype(jnp.bfloat16)).astype(jnp.float32)
    imag_part = lax.optimization_barrier(jnp.imag(values).astype(jnp.bfloat16)).astype(jnp.float32)
    return to_complex(real_part, imag_part)


def reference(facet_strips, subgrid_offsets, sample_cells, sample_values, sample_weights, sample_flags):
    facet_count = FACETS
    col_groups = facet_count // FACET_ROWS
    subgrid_len = SG
    counter = jnp.arange(FN).astype(jnp.float32)
    window = 1.0 + 0.5 * jnp.cos(counter * (2.0 * math.pi / FN))
    positions = (subgrid_offsets[:, :, None] + jnp.arange(CONTRIB, dtype=jnp.int32)[None, None, :]) % FN

    def one_band(running, inputs):
        strips, cell_pairs, observed, weights, flagged = inputs
        cell_index = (cell_pairs[:, :, 0] * subgrid_len + cell_pairs[:, :, 1]).astype(jnp.int32)
        signal = to_complex(strips[:, 0], strips[:, 1]) * window
        spectrum = jnp.fft.fft(signal, axis=-1) * FN ** -0.5
        cutout = spectrum[:, :, positions]
        pieces = rounded(jnp.fft.ifft(cutout, axis=-1) * CONTRIB ** 0.5)
        sky_image = pieces.reshape(col_groups, FACET_ROWS, COLS, FRONTS, facet_count, CONTRIB)
        sky_image = jnp.transpose(sky_image, (3, 4, 0, 2, 1, 5)).reshape(FRONTS, facet_count, col_groups * COLS, subgrid_len)
        model_grid = (jnp.fft.fft(sky_image, axis=-1) * subgrid_len ** -0.5).reshape(FRONTS, facet_count, CELLS)
        predicted = jnp.take_along_axis(model_grid, cell_index, axis=2)
        factor = weights * flagged.astype(jnp.float32)
        residual = to_complex(factor * (observed[:, :, 0] - jnp.real(predicted)), factor * (observed[:, :, 1] - jnp.imag(predicted)))
        slot_index = cell_index + jnp.arange(FRONTS * facet_count, dtype=jnp.int32).reshape(FRONTS, facet_count, 1) * CELLS
        slot_index = slot_index.reshape(-1)
        grid_real = jax.ops.segment_sum(jnp.real(residual).reshape(-1), slot_index, num_segments=FRONTS * facet_count * CELLS)
        grid_imag = jax.ops.segment_sum(jnp.imag(residual).reshape(-1), slot_index, num_segments=FRONTS * facet_count * CELLS)
        grid = to_complex(grid_real, grid_imag).reshape(FRONTS, facet_count, col_groups * COLS, subgrid_len)
        returned = jnp.fft.ifft(grid, axis=-1) * subgrid_len ** 0.5
        returned = returned.reshape(FRONTS, facet_count, col_groups, COLS, FACET_ROWS, CONTRIB)
        returned = jnp.transpose(returned, (2, 4, 3, 0, 1, 5)).reshape(facet_count, COLS, FRONTS, facet_count, CONTRIB)
        return running + rounded(returned), None

    zeros = jnp.zeros((facet_count, COLS, FRONTS, facet_count, CONTRIB), jnp.float32)
    start_value = to_complex(zeros, zeros)
    summed = lax.scan(one_band, start_value, (facet_strips, sample_cells, sample_values, sample_weights, sample_flags))[0]
    partial_value = jnp.fft.fft(summed, axis=-1) * CONTRIB ** -0.5
    spread = jnp.zeros((facet_count, COLS, FN), partial_value.dtype).at[:, :, positions].add(partial_value)
    lines = jnp.fft.ifft(spread, axis=-1) * FN ** 0.5 * window
    return jnp.stack([jnp.real(lines), jnp.imag(lines)], axis=2)
```

```python
import math

import jax
import jax.numpy as jnp
import numpy as np
from jax import lax
from jax.experimental import pallas as pl
from jax.experimental.pallas import tpu as pltpu
from jax.sharding import PartitionSpec as P

FN = 4096
CONTRIB = 64
FACET_ROWS = 8
COLS = 8
FRONTS = 2
SG = 512
VIS = 512
EXACT = lax.Precision.HIGHEST


def unit_table(length, rotation, rows, cols):
    angle = np.outer(np.arange(rows), np.arange(cols)) % length * (2.0 * np.pi / length)
    return np.cos(angle), rotation * np.sin(angle)


def real_form(cosine, sine):
    return np.block([[cosine, sine], [-sine, cosine]])


def f32(x):
    return jnp.asarray(np.asarray(x, np.float32))


def phase_table():
    cosine, sine = unit_table(SG, -1.0, CONTRIB, SG)
    cos8, sin8 = unit_table(8, -1.0, 8, SG)
    table = np.concatenate([cosine, sine, cos8, sin8], axis=0).astype(np.float32)
    high = table.astype(jnp.bfloat16)
    low = (table - high.astype(np.float32)).astype(jnp.bfloat16)
    return jnp.asarray(np.stack([high, low]))


def phase_kernel(table_ref, cells_ref, out_ref):
    for t in range(FRONTS):
        col = cells_ref[t, 1:2, :]
        hot = (lax.broadcasted_iota(jnp.int32, (SG, VIS), 0) == col).astype(jnp.float32)
        hot = hot.astype(jnp.bfloat16)
        out_ref[t] = jnp.dot(
            table_ref[0], hot, preferred_element_type=jnp.float32
        ) + jnp.dot(table_ref[1], hot, preferred_element_type=jnp.float32)


def subgrid_kernel(
    image_ref, phase_ref, cells_ref, values_ref, weights_ref, flags_ref, out_ref
):
    scale = SG ** (-0.5)
    half = CONTRIB
    for t in range(FRONTS):
        row = cells_ref[t, 0:1, :]
        place = lax.broadcasted_iota(jnp.int32, (COLS * 8, VIS), 0)
        hot = (place == row).astype(jnp.float32).astype(jnp.bfloat16)
        turned = (row & 7) * 8 + (row >> 3)
        hot_back = (place == turned).astype(jnp.float32).astype(jnp.bfloat16)
        er = phase_ref[t, 0:half, :]
        ei = phase_ref[t, half : 2 * half, :]
        pred_re = jnp.zeros((1, VIS), jnp.float32)
        pred_im = jnp.zeros((1, VIS), jnp.float32)
        for i in range(FACET_ROWS):
            slab = image_ref[:, i, t].astype(jnp.float32).reshape(COLS * 8, 2 * half)
            slab = slab.astype(jnp.bfloat16)
            picked = lax.dot_general(
                slab, hot, (((0,), (0,)), ((), ())), preferred_element_type=jnp.float32
            )
            pr = picked[:half]
            pi = picked[half:]
            sr = jnp.sum(pr * er - pi * ei, axis=0, keepdims=True)
            si = jnp.sum(pr * ei + pi * er, axis=0, keepdims=True)
            c8 = phase_ref[t, 2 * half + i : 2 * half + i + 1, :]
            s8 = phase_ref[t, 2 * half + 8 + i : 2 * half + 9 + i, :]
            pred_re += c8 * sr - s8 * si
            pred_im += c8 * si + s8 * sr
        factor = weights_ref[t : t + 1, :] * flags_ref[t : t + 1, :].astype(jnp.float32)
        res_re = factor * (values_ref[t, 0:1, :] - scale * pred_re) * scale
        res_im = factor * (values_ref[t, 1:2, :] - scale * pred_im) * scale
        for i in range(FACET_ROWS):
            c8 = phase_ref[t, 2 * half + i : 2 * half + i + 1, :]
            s8 = phase_ref[t, 2 * half + 8 + i : 2 * half + 9 + i, :]
            gr = res_re * c8 + res_im * s8
            gi = res_im * c8 - res_re * s8
            wave = jnp.concatenate([gr * er + gi * ei, gi * er - gr * ei], axis=0)
            back = lax.dot_general(
                hot_back,
                wave.astype(jnp.bfloat16),
                (((1,), (1,)), ((), ())),
                preferred_element_type=jnp.float32,
            )
            out_ref[:, t, 8 * i : 8 * i + 8, :] = back.reshape(COLS, 8, 2 * half).astype(
                jnp.bfloat16
            )


def local(facet_strips, subgrid_offsets, sample_cells, sample_values, sample_weights, sample_flags):
    vmem = pl.BlockSpec(memory_space=pltpu.VMEM)
    facets = lax.axis_size("facet")
    windows = facets * FRONTS
    blocks = FN // CONTRIB
    n = np.arange(FN)
    window = (1.0 + 0.5 * np.cos(2.0 * np.pi * n / FN)) * FN ** (-0.5)
    offsets = jnp.transpose(subgrid_offsets).reshape(windows)
    first = offsets // CONTRIB
    shift = offsets % CONTRIB
    block_index = lax.iota(jnp.int32, blocks)
    pick = jnp.concatenate([first, (first + 1) % blocks])[:, None] == block_index[None, :]
    pick = pick.astype(jnp.float32)
    inside = lax.iota(jnp.int32, CONTRIB)[None, :] >= shift[:, None]
    angle = (shift[:, None] * lax.iota(jnp.int32, CONTRIB)[None, :] % CONTRIB).astype(
        jnp.float32
    ) * (2.0 * math.pi / CONTRIB)
    ramp_cos = jnp.cos(angle)
    ramp_sin = jnp.sin(angle)

    short = real_form(*unit_table(CONTRIB, -1.0, CONTRIB, CONTRIB)).reshape(2, 64, 2, 64)
    turn_cos, turn_sin = unit_table(FN, 1.0, CONTRIB, CONTRIB)
    strips = (facet_strips[0, 0] * f32(window)).reshape(2, COLS, CONTRIB, CONTRIB)
    section = jnp.einsum("rcan,rasp->scpn", strips, f32(short), precision=EXACT)
    tc, ts = f32(turn_cos), f32(turn_sin)
    turned = jnp.stack(
        [section[0] * tc + section[1] * ts, section[1] * tc - section[0] * ts], axis=0
    )
    spectrum = jnp.einsum("rcpn,rnsb->bcsp", turned, f32(short), precision=EXACT)
    chosen = jnp.dot(pick, spectrum.reshape(blocks, -1), precision=EXACT)
    chosen = chosen.reshape(2, windows, COLS * 2, CONTRIB)
    cut = jnp.where(inside[:, None, :], chosen[0], chosen[1]).reshape(windows * COLS, 128)
    plus = real_form(*unit_table(CONTRIB, 1.0, CONTRIB, CONTRIB)) * CONTRIB ** (-0.5)
    plus = np.concatenate([plus, plus[:, 64:], plus[:, :64]], axis=1)
    piece = jnp.dot(cut, f32(plus), precision=lax.Precision.HIGH).reshape(windows, COLS, 256)
    ramp_c = jnp.concatenate([ramp_cos, ramp_cos], axis=1)
    ramp_s = jnp.concatenate([ramp_sin, -ramp_sin], axis=1)
    piece = piece[..., :128] * ramp_c[:, None] + piece[..., 128:] * ramp_s[:, None]
    leaving = piece.astype(jnp.bfloat16).reshape(facets, FRONTS, COLS, 128)
    arrived = lax.all_to_all(leaving, "facet", split_axis=0, concat_axis=0, tiled=True)

    cells = sample_cells.reshape(FRONTS, 2, VIS)
    phases = pl.pallas_call(
        phase_kernel,
        out_shape=jax.ShapeDtypeStruct((FRONTS, 144, VIS), jnp.float32),
        in_specs=[vmem] * 2,
        out_specs=vmem,
        cost_estimate=pl.CostEstimate(
            flops=4 * 144 * SG * VIS * 2, bytes_accessed=1 << 20, transcendentals=0
        ),
    )(phase_table(), cells)
    returned = pl.pallas_call(
        subgrid_kernel,
        out_shape=jax.ShapeDtypeStruct((COLS, FRONTS, facets, 128), jnp.bfloat16),
        in_specs=[vmem] * 6,
        out_specs=vmem,
    )(
        arrived.reshape(facets // FACET_ROWS, FACET_ROWS, FRONTS, COLS, 128),
        phases,
        cells,
        sample_values.reshape(FRONTS, 2, VIS),
        sample_weights.reshape(FRONTS, VIS),
        sample_flags.reshape(FRONTS, VIS),
    )

    banded = lax.all_to_all(returned, "band", split_axis=0, concat_axis=0, tiled=True)
    summed = jnp.sum(banded.astype(jnp.float32), axis=0)
    summed = summed.reshape(FRONTS, FACET_ROWS, facets // FACET_ROWS, 128)
    summed = jnp.transpose(summed, (2, 1, 0, 3)).reshape(facets, FRONTS, 128)
    delivered = lax.all_to_all(
        summed.astype(jnp.bfloat16), "facet", split_axis=0, concat_axis=0, tiled=True
    )
    delivered = delivered.astype(jnp.float32).reshape(windows, 2, CONTRIB)
    dr, di = delivered[:, 0], delivered[:, 1]
    aligned = jnp.concatenate(
        [dr * ramp_cos - di * ramp_sin, di * ramp_cos + dr * ramp_sin], axis=1
    )
    minus = short.reshape(128, 128) * CONTRIB ** (-0.5)
    partial = jnp.dot(aligned, f32(minus), precision=EXACT)
    inside2 = jnp.concatenate([inside, inside], axis=1)
    masked = jnp.concatenate(
        [jnp.where(inside2, partial, 0.0), jnp.where(inside2, 0.0, partial)], axis=0
    )
    spread = lax.dot_general(pick, masked, (((0,), (0,)), ((), ())), precision=EXACT)
    spread = spread.reshape(blocks, 2, CONTRIB)
    plus4 = real_form(*unit_table(CONTRIB, 1.0, CONTRIB, CONTRIB)).reshape(2, 64, 2, 64)
    line = jnp.einsum("brp,rbsn->spn", spread, f32(plus4), precision=EXACT)
    line = jnp.stack([line[0] * tc - line[1] * ts, line[1] * tc + line[0] * ts], axis=0)
    line = jnp.einsum("rpn,rpsa->san", line, f32(plus4), precision=EXACT)
    result = line.reshape(2, FN) * f32(window)
    return result[None, None]


def solution(mesh):
    placed = (
        P("band", "facet", None, None, None),
        P(),
        P("band", None, "facet", None, None),
        P("band", None, "facet", None, None),
        P("band", None, "facet", None),
        P("band", None, "facet", None),
    )
    return jax.shard_map(
        local, mesh=mesh, in_specs=placed, out_specs=P("facet", "band", None, None), check_vma=False
    )
```

```python
import math

import jax
import jax.numpy as jnp
import numpy as np
from jax import lax
from jax.experimental import pallas as pl
from jax.experimental.pallas import tpu as pltpu
from jax.sharding import PartitionSpec as P

FN = 4096
CONTRIB = 64
FACET_ROWS = 8
COLS = 8
FRONTS = 2
SG = 512
VIS = 512
EXACT = lax.Precision.HIGHEST


def unit_table(length, rotation, rows, cols):
    angle = np.outer(np.arange(rows), np.arange(cols)) % length * (2.0 * np.pi / length)
    return np.cos(angle), rotation * np.sin(angle)


def real_form(cosine, sine):
    return np.block([[cosine, sine], [-sine, cosine]])


def f32(x):
    return jnp.asarray(np.asarray(x, np.float32))


def phase_table():
    cosine, sine = unit_table(SG, -1.0, CONTRIB, SG)
    cos8, sin8 = unit_table(8, -1.0, 8, SG)
    table = np.concatenate([cosine, sine, cos8, sin8], axis=0).astype(np.float32)
    high = table.astype(jnp.bfloat16)
    low = (table - high.astype(np.float32)).astype(jnp.bfloat16)
    return jnp.asarray(np.stack([high, low]))


def exchange_kernel(
    leaving_ref,
    table_ref,
    cells_ref,
    values_ref,
    weights_ref,
    flags_ref,
    out_ref,
    arrived_ref,
    phase_ref,
    back_ref,
    banded_ref,
    sum_ref,
    landed_ref,
    sems,
):
    facets = leaving_ref.shape[0]
    bands = back_ref.shape[0]
    groups = facets // FACET_ROWS
    me = lax.axis_index("facet")
    band = lax.axis_index("band")

    barrier = pltpu.get_barrier_semaphore()

    @pl.loop(1, facets)
    def _(k):
        pl.semaphore_signal(
            barrier, inc=1, device_id={"facet": lax.rem(me + k, facets)},
            device_id_type=pl.DeviceIdType.MESH,
        )

    @pl.loop(1, bands)
    def _(k):
        pl.semaphore_signal(
            barrier, inc=1, device_id={"band": lax.rem(band + k, bands)},
            device_id_type=pl.DeviceIdType.MESH,
        )

    pl.semaphore_wait(barrier, facets + bands - 2)

    def whole(ref, count, sem):
        part = ref.at[pl.ds(0, count)]
        pltpu.make_async_copy(part, part, sem).wait()

    own = pltpu.make_async_copy(leaving_ref.at[me], arrived_ref.at[me], sems.at[2])
    own.start()

    @pl.loop(1, facets)
    def _(k):
        to = lax.rem(me + 27 * k, facets)
        pltpu.make_async_remote_copy(
            src_ref=leaving_ref.at[to],
            dst_ref=arrived_ref.at[me],
            send_sem=sems.at[0],
            recv_sem=sems.at[1],
            device_id={"facet": to},
            device_id_type=pl.DeviceIdType.MESH,
        ).start()

    for t in range(FRONTS):
        col = cells_ref[t, 1:2, :]
        hot = (lax.broadcasted_iota(jnp.int32, (SG, VIS), 0) == col).astype(jnp.float32)
        hot = hot.astype(jnp.bfloat16)
        phase_ref[t] = jnp.dot(
            table_ref[0], hot, preferred_element_type=jnp.float32
        ) + jnp.dot(table_ref[1], hot, preferred_element_type=jnp.float32)
    own.wait()
    whole(leaving_ref, facets - 1, sems.at[0])
    whole(arrived_ref, facets - 1, sems.at[1])

    scale = SG ** (-0.5)
    half = CONTRIB
    for t in range(FRONTS):
        row = cells_ref[t, 0:1, :]
        place = lax.broadcasted_iota(jnp.int32, (COLS * groups, VIS), 0)
        hot = (place == row).astype(jnp.float32).astype(jnp.bfloat16)
        turned = (row & 7) * groups + (row >> 3)
        hot_back = (place == turned).astype(jnp.float32).astype(jnp.bfloat16)
        er = phase_ref[t, 0:half, :]
        ei = phase_ref[t, half : 2 * half, :]
        pred_re = jnp.zeros((1, VIS), jnp.float32)
        pred_im = jnp.zeros((1, VIS), jnp.float32)
        for i in range(FACET_ROWS):
            slab = jnp.concatenate(
                [
                    arrived_ref[FACET_ROWS * j + i, t].astype(jnp.float32)
                    for j in range(groups)
                ],
                axis=0,
            ).astype(jnp.bfloat16)
            picked = lax.dot_general(
                slab, hot, (((0,), (0,)), ((), ())), preferred_element_type=jnp.float32
            )
            pr = picked[:half]
            pi = picked[half:]
            sr = jnp.sum(pr * er - pi * ei, axis=0, keepdims=True)
            si = jnp.sum(pr * ei + pi * er, axis=0, keepdims=True)
            c8 = phase_ref[t, 2 * half + i : 2 * half + i + 1, :]
            s8 = phase_ref[t, 2 * half + 8 + i : 2 * half + 9 + i, :]
            pred_re += c8 * sr - s8 * si
            pred_im += c8 * si + s8 * sr
        factor = weights_ref[t : t + 1, :] * flags_ref[t : t + 1, :].astype(jnp.float32)
        res_re = factor * (values_ref[t, 0:1, :] - scale * pred_re) * scale
        res_im = factor * (values_ref[t, 1:2, :] - scale * pred_im) * scale
        for i in range(FACET_ROWS):
            c8 = phase_ref[t, 2 * half + i : 2 * half + i + 1, :]
            s8 = phase_ref[t, 2 * half + 8 + i : 2 * half + 9 + i, :]
            gr = res_re * c8 + res_im * s8
            gi = res_im * c8 - res_re * s8
            wave = jnp.concatenate([gr * er + gi * ei, gi * er - gr * ei], axis=0)
            back = lax.dot_general(
                hot_back,
                wave.astype(jnp.bfloat16),
                (((1,), (1,)), ((), ())),
                preferred_element_type=jnp.float32,
            )
            back_ref[:, t, groups * i : groups * (i + 1), :] = back.reshape(
                COLS, groups, 2 * half
            ).astype(jnp.bfloat16)

    own = pltpu.make_async_copy(back_ref.at[band], banded_ref.at[band], sems.at[5])
    own.start()

    @pl.loop(1, bands)
    def _(k):
        to = lax.rem(band + k, bands)
        pltpu.make_async_remote_copy(
            src_ref=back_ref.at[to],
            dst_ref=banded_ref.at[band],
            send_sem=sems.at[3],
            recv_sem=sems.at[4],
            device_id={"band": to},
            device_id_type=pl.DeviceIdType.MESH,
        ).start()

    own.wait()
    whole(back_ref, bands - 1, sems.at[3])
    whole(banded_ref, bands - 1, sems.at[4])
    for t in range(FRONTS):
        total = banded_ref[0, t].astype(jnp.float32)
        for b in range(1, bands):
            total += banded_ref[b, t].astype(jnp.float32)
        sum_ref[:, t, :] = total

    mine = lax.rem(me, FACET_ROWS) * groups + me // FACET_ROWS
    own = pltpu.make_async_copy(sum_ref.at[mine], landed_ref.at[me], sems.at[8])
    own.start()

    @pl.loop(1, facets)
    def _(k):
        to = lax.rem(me + 27 * k, facets)
        slot = lax.rem(to, FACET_ROWS) * groups + to // FACET_ROWS
        pltpu.make_async_remote_copy(
            src_ref=sum_ref.at[slot],
            dst_ref=landed_ref.at[me],
            send_sem=sems.at[6],
            recv_sem=sems.at[7],
            device_id={"facet": to},
            device_id_type=pl.DeviceIdType.MESH,
        ).start()

    own.wait()
    whole(sum_ref, facets - 1, sems.at[6])
    whole(landed_ref, facets - 1, sems.at[7])
    out_ref[...] = landed_ref[...]


def local(facet_strips, subgrid_offsets, sample_cells, sample_values, sample_weights, sample_flags):
    vmem = pl.BlockSpec(memory_space=pltpu.VMEM)
    facets = lax.axis_size("facet")
    windows = facets * FRONTS
    blocks = FN // CONTRIB
    n = np.arange(FN)
    window = (1.0 + 0.5 * np.cos(2.0 * np.pi * n / FN)) * FN ** (-0.5)
    offsets = jnp.transpose(subgrid_offsets).reshape(windows)
    first = offsets // CONTRIB
    shift = offsets % CONTRIB
    block_index = lax.iota(jnp.int32, blocks)
    pick = jnp.concatenate([first, (first + 1) % blocks])[:, None] == block_index[None, :]
    pick = pick.astype(jnp.float32)
    inside = lax.iota(jnp.int32, CONTRIB)[None, :] >= shift[:, None]
    angle = (shift[:, None] * lax.iota(jnp.int32, CONTRIB)[None, :] % CONTRIB).astype(
        jnp.float32
    ) * (2.0 * math.pi / CONTRIB)
    ramp_cos = jnp.cos(angle)
    ramp_sin = jnp.sin(angle)

    short = real_form(*unit_table(CONTRIB, -1.0, CONTRIB, CONTRIB)).reshape(2, 64, 2, 64)
    turn_cos, turn_sin = unit_table(FN, 1.0, CONTRIB, CONTRIB)
    strips = (facet_strips[0, 0] * f32(window)).reshape(2, COLS, CONTRIB, CONTRIB)
    section = jnp.einsum("rcan,rasp->scpn", strips, f32(short), precision=EXACT)
    tc, ts = f32(turn_cos), f32(turn_sin)
    turned = jnp.stack(
        [section[0] * tc + section[1] * ts, section[1] * tc - section[0] * ts], axis=0
    )
    spectrum = jnp.einsum("rcpn,rnsb->bcsp", turned, f32(short), precision=EXACT)
    chosen = jnp.dot(pick, spectrum.reshape(blocks, -1), precision=EXACT)
    chosen = chosen.reshape(2, windows, COLS * 2, CONTRIB)
    cut = jnp.where(inside[:, None, :], chosen[0], chosen[1]).reshape(windows * COLS, 128)
    plus = real_form(*unit_table(CONTRIB, 1.0, CONTRIB, CONTRIB)) * CONTRIB ** (-0.5)
    plus = np.concatenate([plus, plus[:, 64:], plus[:, :64]], axis=1)
    piece = jnp.dot(cut, f32(plus), precision=lax.Precision.HIGH).reshape(windows, COLS, 256)
    ramp_c = jnp.concatenate([ramp_cos, ramp_cos], axis=1)
    ramp_s = jnp.concatenate([ramp_sin, -ramp_sin], axis=1)
    piece = piece[..., :128] * ramp_c[:, None] + piece[..., 128:] * ramp_s[:, None]
    leaving = piece.astype(jnp.bfloat16).reshape(facets, FRONTS, COLS, 128)

    bands = lax.axis_size("band")
    delivered = pl.pallas_call(
        exchange_kernel,
        out_shape=jax.ShapeDtypeStruct((facets, FRONTS, 128), jnp.float32),
        in_specs=[vmem] * 6,
        out_specs=vmem,
        scratch_shapes=[
            pltpu.VMEM((facets, FRONTS, COLS, 128), jnp.bfloat16),
            pltpu.VMEM((FRONTS, 144, VIS), jnp.float32),
            pltpu.VMEM((bands, FRONTS, facets, 128), jnp.bfloat16),
            pltpu.VMEM((bands, FRONTS, facets, 128), jnp.bfloat16),
            pltpu.VMEM((facets, FRONTS, 128), jnp.float32),
            pltpu.VMEM((facets, FRONTS, 128), jnp.float32),
            pltpu.SemaphoreType.DMA((9,)),
        ],
        compiler_params=pltpu.CompilerParams(collective_id=0, has_side_effects=True),
    )(
        leaving,
        phase_table(),
        sample_cells.reshape(FRONTS, 2, VIS),
        sample_values.reshape(FRONTS, 2, VIS),
        sample_weights.reshape(FRONTS, VIS),
        sample_flags.reshape(FRONTS, VIS),
    )
    delivered = delivered.reshape(windows, 2, CONTRIB)
    dr, di = delivered[:, 0], delivered[:, 1]
    aligned = jnp.concatenate(
        [dr * ramp_cos - di * ramp_sin, di * ramp_cos + dr * ramp_sin], axis=1
    )
    minus = short.reshape(128, 128) * CONTRIB ** (-0.5)
    partial = jnp.dot(aligned, f32(minus), precision=EXACT)
    inside2 = jnp.concatenate([inside, inside], axis=1)
    masked = jnp.concatenate(
        [jnp.where(inside2, partial, 0.0), jnp.where(inside2, 0.0, partial)], axis=0
    )
    spread = lax.dot_general(pick, masked, (((0,), (0,)), ((), ())), precision=EXACT)
    spread = spread.reshape(blocks, 2, CONTRIB)
    plus4 = real_form(*unit_table(CONTRIB, 1.0, CONTRIB, CONTRIB)).reshape(2, 64, 2, 64)
    line = jnp.einsum("brp,rbsn->spn", spread, f32(plus4), precision=EXACT)
    line = jnp.stack([line[0] * tc - line[1] * ts, line[1] * tc + line[0] * ts], axis=0)
    line = jnp.einsum("rpn,rpsa->san", line, f32(plus4), precision=EXACT)
    result = line.reshape(2, FN) * f32(window)
    return result[None, None]


def solution(mesh):
    placed = (
        P("band", "facet", None, None, None),
        P(),
        P("band", None, "facet", None, None),
        P("band", None, "facet", None, None),
        P("band", None, "facet", None),
        P("band", None, "facet", None),
    )
    return jax.shard_map(
        local, mesh=mesh, in_specs=placed, out_specs=P("facet", "band", None, None), check_vma=False
    )
```

```python
import math

import jax
import jax.numpy as jnp
import numpy as np
from jax import lax
from jax.experimental import pallas as pl
from jax.experimental.pallas import tpu as pltpu
from jax.sharding import PartitionSpec as P

FN = 4096
CONTRIB = 64
FACET_ROWS = 8
COLS = 8
FRONTS = 2
SG = 512
VIS = 512
EXACT = lax.Precision.HIGHEST


def unit_table(length, rotation, rows, cols):
    angle = np.outer(np.arange(rows), np.arange(cols)) % length * (2.0 * np.pi / length)
    return np.cos(angle), rotation * np.sin(angle)


def real_form(cosine, sine):
    return np.block([[cosine, sine], [-sine, cosine]])


def f32(x):
    return jnp.asarray(np.asarray(x, np.float32))


def phase_table():
    cosine, sine = unit_table(SG, -1.0, CONTRIB, SG)
    cos8, sin8 = unit_table(8, -1.0, 8, SG)
    table = np.concatenate([cosine, sine, cos8, sin8], axis=0).astype(np.float32)
    high = table.astype(jnp.bfloat16)
    low = (table - high.astype(np.float32)).astype(jnp.bfloat16)
    return jnp.asarray(np.stack([high, low]))


def swapped(x):
    return jnp.concatenate([x[:, CONTRIB:], x[:, :CONTRIB]], axis=1)


def exact_dot(left, right, left_dim=1, right_dim=0):
    return lax.dot_general(
        left,
        right,
        (((left_dim,), (right_dim,)), ((), ())),
        precision=EXACT,
        preferred_element_type=jnp.float32,
    )


def major_kernel(
    strips_ref,
    offsets_ref,
    offsets_row_ref,
    tables_ref,
    turn_ref,
    window_ref,
    table_ref,
    cells_ref,
    values_ref,
    weights_ref,
    flags_ref,
    out_ref,
    staged_ref,
    leaving_ref,
    arrived_ref,
    phase_ref,
    back_ref,
    banded_ref,
    sum_ref,
    landed_ref,
    sems,
):
    facets = leaving_ref.shape[1]
    bands = back_ref.shape[1]
    groups = facets // FACET_ROWS
    windows = facets * FRONTS
    half = CONTRIB
    blocks = FN // CONTRIB
    me = lax.axis_index("facet")
    band = lax.axis_index("band")

    barrier = pltpu.get_barrier_semaphore()

    @pl.loop(1, facets)
    def _(k):
        pl.semaphore_signal(
            barrier, inc=1, device_id={"facet": lax.rem(me + 27 * k, facets)},
            device_id_type=pl.DeviceIdType.MESH,
        )

    @pl.loop(1, bands)
    def _(k):
        pl.semaphore_signal(
            barrier, inc=1, device_id={"band": lax.rem(band + k, bands)},
            device_id_type=pl.DeviceIdType.MESH,
        )

    offsets = offsets_ref[...]
    first = offsets >> 6
    shift = offsets & (half - 1)
    lane = lax.broadcasted_iota(jnp.int32, (windows, 2 * half), 1) & (half - 1)
    inside = lane >= shift
    angle = ((shift * lane) & (half - 1)).astype(jnp.float32) * (2.0 * math.pi / half)
    ramp_c = jnp.cos(angle)
    ramp_s = jnp.sin(angle)
    left_half = lax.broadcasted_iota(jnp.int32, (windows, 2 * half), 1) < half
    ramp_s = jnp.where(left_half, ramp_s, -ramp_s)
    block = lax.broadcasted_iota(jnp.int32, (windows, blocks), 1)
    pick = jnp.concatenate(
        [
            (block == first).astype(jnp.float32),
            (block == ((first + 1) & (blocks - 1))).astype(jnp.float32),
        ],
        axis=0,
    )
    section = exact_dot(tables_ref[0], strips_ref[...])
    tc = turn_ref[0]
    ts = turn_ref[1]
    turned_re = section[:half] * tc + section[half:] * ts
    turned_im = section[half:] * tc - section[:half] * ts
    for c in range(COLS):
        part = slice(half * c, half * (c + 1))
        pair = jnp.concatenate([turned_re[:, part], turned_im[:, part]], axis=1)
        spec = exact_dot(tables_ref[0], pair, 1, 1)
        spec = jnp.concatenate([spec[:half], spec[half:]], axis=1)
        chosen = exact_dot(pick, spec)
        cut = jnp.where(inside, chosen[:windows], chosen[windows:])
        piece = exact_dot(cut, tables_ref[1])
        piece = piece * ramp_c + swapped(piece) * ramp_s
        for t in range(FRONTS):
            staged_ref[t, :, c, :] = piece[facets * t : facets * (t + 1)]
    leaving_ref[...] = staged_ref[...].astype(jnp.bfloat16)

    pl.semaphore_wait(barrier, facets + bands - 2)

    def whole(ref, count, sem):
        part = ref.at[pl.ds(0, count)]
        pltpu.make_async_copy(part, part, sem).wait()

    owns = []
    for t in range(FRONTS):
        own = pltpu.make_async_copy(
            leaving_ref.at[t, me], arrived_ref.at[t, me], sems.at[8 + t]
        )
        own.start()
        owns.append(own)

        @pl.loop(1, facets)
        def _(k):
            to = lax.rem(me + 27 * k, facets)
            pltpu.make_async_remote_copy(
                src_ref=leaving_ref.at[t, to],
                dst_ref=arrived_ref.at[t, me],
                send_sem=sems.at[t],
                recv_sem=sems.at[2 + t],
                device_id={"facet": to},
                device_id_type=pl.DeviceIdType.MESH,
            ).start()

    for t in range(FRONTS):
        col = cells_ref[t, 1:2, :]
        hot = (lax.broadcasted_iota(jnp.int32, (SG, VIS), 0) == col).astype(jnp.float32)
        hot = hot.astype(jnp.bfloat16)
        phase_ref[t] = jnp.dot(
            table_ref[0], hot, preferred_element_type=jnp.float32
        ) + jnp.dot(table_ref[1], hot, preferred_element_type=jnp.float32)
    scale = SG ** (-0.5)
    returns = []
    for t in range(FRONTS):
        owns[t].wait()
        whole(leaving_ref.at[t], facets - 1, sems.at[t])
        whole(arrived_ref.at[t], facets - 1, sems.at[2 + t])
        row = cells_ref[t, 0:1, :]
        place = lax.broadcasted_iota(jnp.int32, (COLS * groups, VIS), 0)
        hot = (place == row).astype(jnp.float32).astype(jnp.bfloat16)
        turned = (row & 7) * groups + (row >> 3)
        hot_back = (place == turned).astype(jnp.float32).astype(jnp.bfloat16)
        er = phase_ref[t, 0:half, :]
        ei = phase_ref[t, half : 2 * half, :]
        pred_re = jnp.zeros((1, VIS), jnp.float32)
        pred_im = jnp.zeros((1, VIS), jnp.float32)
        for i in range(FACET_ROWS):
            slab = jnp.concatenate(
                [
                    arrived_ref[t, FACET_ROWS * j + i].astype(jnp.float32)
                    for j in range(groups)
                ],
                axis=0,
            ).astype(jnp.bfloat16)
            picked = lax.dot_general(
                slab, hot, (((0,), (0,)), ((), ())), preferred_element_type=jnp.float32
            )
            pr = picked[:half]
            pi = picked[half:]
            sr = jnp.sum(pr * er - pi * ei, axis=0, keepdims=True)
            si = jnp.sum(pr * ei + pi * er, axis=0, keepdims=True)
            c8 = phase_ref[t, 2 * half + i : 2 * half + i + 1, :]
            s8 = phase_ref[t, 2 * half + 8 + i : 2 * half + 9 + i, :]
            pred_re += c8 * sr - s8 * si
            pred_im += c8 * si + s8 * sr
        factor = weights_ref[t : t + 1, :] * flags_ref[t : t + 1, :].astype(jnp.float32)
        res_re = factor * (values_ref[t, 0:1, :] - scale * pred_re) * scale
        res_im = factor * (values_ref[t, 1:2, :] - scale * pred_im) * scale
        for i in range(FACET_ROWS):
            c8 = phase_ref[t, 2 * half + i : 2 * half + i + 1, :]
            s8 = phase_ref[t, 2 * half + 8 + i : 2 * half + 9 + i, :]
            gr = res_re * c8 + res_im * s8
            gi = res_im * c8 - res_re * s8
            wave = jnp.concatenate([gr * er + gi * ei, gi * er - gr * ei], axis=0)
            back = lax.dot_general(
                hot_back,
                wave.astype(jnp.bfloat16),
                (((1,), (1,)), ((), ())),
                preferred_element_type=jnp.float32,
            )
            back_ref[t, :, groups * i : groups * (i + 1), :] = back.reshape(
                COLS, groups, 2 * half
            ).astype(jnp.bfloat16)

        own = pltpu.make_async_copy(
            back_ref.at[t, band], banded_ref.at[t, band], sems.at[10 + t]
        )
        own.start()
        returns.append(own)

        @pl.loop(1, bands)
        def _(k):
            to = lax.rem(band + k, bands)
            pltpu.make_async_remote_copy(
                src_ref=back_ref.at[t, to],
                dst_ref=banded_ref.at[t, band],
                send_sem=sems.at[4 + t],
                recv_sem=sems.at[6 + t],
                device_id={"band": to},
                device_id_type=pl.DeviceIdType.MESH,
            ).start()

    for t in range(FRONTS):
        returns[t].wait()
        whole(back_ref.at[t], bands - 1, sems.at[4 + t])
        whole(banded_ref.at[t], bands - 1, sems.at[6 + t])
        total = banded_ref[t, 0].astype(jnp.float32)
        for b in range(1, bands):
            total += banded_ref[t, b].astype(jnp.float32)
        sum_ref[:, t, :] = total

    mine = lax.rem(me, FACET_ROWS) * groups + me // FACET_ROWS
    own = pltpu.make_async_copy(sum_ref.at[mine], landed_ref.at[me], sems.at[14])
    own.start()

    @pl.loop(1, facets)
    def _(k):
        to = lax.rem(me + 27 * k, facets)
        slot = lax.rem(to, FACET_ROWS) * groups + to // FACET_ROWS
        pltpu.make_async_remote_copy(
            src_ref=sum_ref.at[slot],
            dst_ref=landed_ref.at[me],
            send_sem=sems.at[12],
            recv_sem=sems.at[13],
            device_id={"facet": to},
            device_id_type=pl.DeviceIdType.MESH,
        ).start()

    own.wait()
    whole(sum_ref, facets - 1, sems.at[12])
    whole(landed_ref, facets - 1, sems.at[13])

    delivered = jnp.concatenate([landed_ref[:, t, :] for t in range(FRONTS)], axis=0)
    aligned = delivered * ramp_c - swapped(delivered) * ramp_s
    partial = exact_dot(aligned, tables_ref[2])
    first_row = offsets_row_ref[...] >> 6
    block_row = lax.broadcasted_iota(jnp.int32, (blocks, windows), 0)
    here = (block_row == first_row).astype(jnp.float32)
    after = (block_row == ((first_row + 1) & (blocks - 1))).astype(jnp.float32)
    spread = exact_dot(here, jnp.where(inside, partial, 0.0)) + exact_dot(
        after, jnp.where(inside, 0.0, partial)
    )
    both = exact_dot(tables_ref[3][:, :blocks], spread)
    crossed = swapped(both[half:])
    left_half = left_half[:half]
    line = both[:half] + jnp.where(left_half, -crossed, crossed)
    tc2 = tc[:, : 2 * half]
    ts2 = ts[:, : 2 * half]
    line = line * tc2 + swapped(line) * jnp.where(left_half, -ts2, ts2)
    out_ref[...] = exact_dot(tables_ref[4], line, 1, 1) * window_ref[...]


def local(facet_strips, subgrid_offsets, sample_cells, sample_values, sample_weights, sample_flags):
    vmem = pl.BlockSpec(memory_space=pltpu.VMEM)
    facets = lax.axis_size("facet")
    bands = lax.axis_size("band")
    windows = facets * FRONTS
    n = np.arange(FN)
    window = (1.0 + 0.5 * np.cos(2.0 * np.pi * n / FN)) * FN ** (-0.5)
    window = window.reshape(CONTRIB, CONTRIB)
    minus = real_form(*unit_table(CONTRIB, -1.0, CONTRIB, CONTRIB))
    plus = real_form(*unit_table(CONTRIB, 1.0, CONTRIB, CONTRIB))
    short = CONTRIB ** (-0.5)
    cosine, sine = unit_table(CONTRIB, 1.0, CONTRIB, CONTRIB)
    stacked = np.zeros((128, 128))
    stacked[:64, :64] = cosine
    stacked[64:, :64] = sine
    tables = np.stack([minus.T, plus * short, minus * short, stacked, plus.T])
    turn = np.stack([np.tile(x, (1, COLS)) for x in unit_table(FN, 1.0, CONTRIB, CONTRIB)])
    strips = facet_strips[0, 0].reshape(2, COLS, CONTRIB, CONTRIB) * f32(window)
    strips = jnp.transpose(strips, (0, 2, 1, 3)).reshape(2 * CONTRIB, COLS * CONTRIB)
    lines = pl.pallas_call(
        major_kernel,
        out_shape=jax.ShapeDtypeStruct((2 * CONTRIB, CONTRIB), jnp.float32),
        in_specs=[vmem] * 11,
        out_specs=vmem,
        scratch_shapes=[
            pltpu.VMEM((FRONTS, facets, COLS, 128), jnp.float32),
            pltpu.VMEM((FRONTS, facets, COLS, 128), jnp.bfloat16),
            pltpu.VMEM((FRONTS, facets, COLS, 128), jnp.bfloat16),
            pltpu.VMEM((FRONTS, 144, VIS), jnp.float32),
            pltpu.VMEM((FRONTS, bands, facets, 128), jnp.bfloat16),
            pltpu.VMEM((FRONTS, bands, facets, 128), jnp.bfloat16),
            pltpu.VMEM((facets, FRONTS, 128), jnp.float32),
            pltpu.VMEM((facets, FRONTS, 128), jnp.float32),
            pltpu.SemaphoreType.DMA((15,)),
        ],
        compiler_params=pltpu.CompilerParams(collective_id=0, has_side_effects=True),
    )(
        strips,
        subgrid_offsets.reshape(windows, 1),
        subgrid_offsets.reshape(1, windows),
        f32(tables),
        f32(turn),
        f32(np.concatenate([window, window], axis=0)),
        phase_table(),
        sample_cells.reshape(FRONTS, 2, VIS),
        sample_values.reshape(FRONTS, 2, VIS),
        sample_weights.reshape(FRONTS, VIS),
        sample_flags.reshape(FRONTS, VIS),
    )
    return lines.reshape(1, 1, 2, FN)


def solution(mesh):
    placed = (
        P("band", "facet", None, None, None),
        P(),
        P("band", None, "facet", None, None),
        P("band", None, "facet", None, None),
        P("band", None, "facet", None),
        P("band", None, "facet", None),
    )
    return jax.shard_map(
        local, mesh=mesh, in_specs=placed, out_specs=P("facet", "band", None, None), check_vma=False
    )
```

```python
import math

import jax
import jax.numpy as jnp
import numpy as np
from jax import lax
from jax.experimental import pallas as pl
from jax.experimental.pallas import tpu as pltpu
from jax.sharding import PartitionSpec as P

FN = 4096
CONTRIB = 64
FACET_ROWS = 8
COLS = 8
FRONTS = 2
SG = 512
VIS = 512
ROW = 4
DEEP = 8
EXACT = lax.Precision.HIGHEST


def unit_table(length, rotation, rows, cols):
    angle = np.outer(np.arange(rows), np.arange(cols)) % length * (2.0 * np.pi / length)
    return np.cos(angle), rotation * np.sin(angle)


def real_form(cosine, sine):
    return np.block([[cosine, sine], [-sine, cosine]])


def f32(x):
    return jnp.asarray(np.asarray(x, np.float32))


def phase_table():
    cosine, sine = unit_table(SG, -1.0, CONTRIB, SG)
    cos8, sin8 = unit_table(8, -1.0, 8, SG)
    table = np.concatenate([cosine, sine, cos8, sin8], axis=0).astype(np.float32)
    high = table.astype(jnp.bfloat16)
    low = (table - high.astype(np.float32)).astype(jnp.bfloat16)
    return jnp.asarray(np.stack([high, low]))


def swapped(x):
    return jnp.concatenate([x[:, CONTRIB:], x[:, :CONTRIB]], axis=1)


def exact_dot(left, right, left_dim=1, right_dim=0):
    return lax.dot_general(
        left,
        right,
        (((left_dim,), (right_dim,)), ((), ())),
        precision=EXACT,
        preferred_element_type=jnp.float32,
    )


def split_index(facet, deep):
    across = facet // (ROW * deep) * ROW + facet % ROW
    return across, facet // ROW % deep


def major_kernel(
    strips_ref,
    offsets_ref,
    tables_ref,
    split_ref,
    turn_ref,
    window_ref,
    table_ref,
    cells_ref,
    values_ref,
    weights_ref,
    flags_ref,
    out_ref,
    strip_ref,
    staged_ref,
    leaving_ref,
    middle_ref,
    arrived_ref,
    phase_ref,
    back_ref,
    banded_ref,
    sum_ref,
    passing_ref,
    landed_ref,
    placed_ref,
    sems,
):
    deep = leaving_ref.shape[1]
    wide = leaving_ref.shape[2]
    facets = deep * wide
    bands = back_ref.shape[1]
    groups = facets // FACET_ROWS
    windows = facets * FRONTS
    half = CONTRIB
    blocks = FN // CONTRIB
    me = lax.axis_index("facet")
    band = lax.axis_index("band")
    z = lax.rem(me // ROW, deep)
    w = me // (ROW * deep) * ROW + lax.rem(me, ROW)

    def along_z(to):
        return {"facet": (w // ROW * deep + to) * ROW + lax.rem(w, ROW)}

    def along_w(to):
        return {"facet": (to // ROW * deep + z) * ROW + lax.rem(to, ROW)}

    def along_band(to):
        return {"band": to}

    ways = ((z, deep, along_z), (w, wide, along_w), (band, bands, along_band))

    barrier = pltpu.get_barrier_semaphore()

    for mine, count, device in ways:

        @pl.loop(1, count)
        def _(k):
            pl.semaphore_signal(
                barrier, inc=1, device_id=device(lax.rem(mine + k, count)),
                device_id_type=pl.DeviceIdType.MESH,
            )

    line_index = lax.broadcasted_iota(jnp.int32, (facets, facets), 0)
    diagonal = line_index == lax.broadcasted_iota(jnp.int32, (facets, facets), 1)
    offsets = jnp.concatenate(
        [
            jnp.sum(jnp.where(diagonal, offsets_ref[t : t + 1, :], 0), axis=1, keepdims=True)
            for t in range(FRONTS)
        ],
        axis=0,
    )
    first = offsets >> 6
    shift = offsets & (half - 1)
    lane = lax.broadcasted_iota(jnp.int32, (windows, 2 * half), 1) & (half - 1)
    inside = lane >= shift
    angle = ((shift * lane) & (half - 1)).astype(jnp.float32) * (2.0 * math.pi / half)
    ramp_c = jnp.cos(angle)
    ramp_s = jnp.sin(angle)
    left_half = lax.broadcasted_iota(jnp.int32, (windows, 2 * half), 1) < half
    ramp_s = jnp.where(left_half, ramp_s, -ramp_s)
    block = lax.broadcasted_iota(jnp.int32, (windows, blocks), 1)
    pick = jnp.concatenate(
        [
            (block == first).astype(jnp.float32),
            (block == ((first + 1) & (blocks - 1))).astype(jnp.float32),
        ],
        axis=0,
    )
    chunks = FN // 128
    for r in range(2):
        for a in range(chunks):
            strip_ref[chunks * r + a] = strips_ref[r, :, 128 * a : 128 * (a + 1)]
    tc2 = turn_ref[0]
    ts2 = turn_ref[1]
    tc = tc2[:, :half]
    ts = ts2[:, :half]
    for c in range(COLS):
        section = exact_dot(split_ref[...], strip_ref[:, c, :] * window_ref[...])
        section = section[:128] + swapped(section[128:])
        section = section[:, :half]
        pair = jnp.concatenate(
            [
                section[:half] * tc + section[half:] * ts,
                section[half:] * tc - section[:half] * ts,
            ],
            axis=1,
        )
        spec = exact_dot(tables_ref[0], pair, 1, 1)
        spec = jnp.concatenate([spec[:half], spec[half:]], axis=1)
        chosen = exact_dot(pick, spec)
        cut = jnp.where(inside, chosen[:windows], chosen[windows:])
        piece = exact_dot(cut, tables_ref[1])
        piece = piece * ramp_c + swapped(piece) * ramp_s
        for t in range(FRONTS):
            staged_ref[t, :, c, :] = piece[facets * t : facets * (t + 1)]
    for t in range(FRONTS):
        for a in range(facets // ROW):
            leaving_ref[t, a % deep, a // deep * ROW : (a // deep + 1) * ROW] = staged_ref[
                t, ROW * a : ROW * (a + 1)
            ].astype(jnp.bfloat16)

    pl.semaphore_wait(barrier, deep + wide + bands - 3)

    def whole(ref, count, sem):
        part = ref.at[pl.ds(0, count)]
        pltpu.make_async_copy(part, part, sem).wait()

    def begin(way, source, target, base):
        mine, count, device = way
        own = pltpu.make_async_copy(source(mine), target, sems.at[base + 2])
        own.start()

        @pl.loop(1, count)
        def _(k):
            to = lax.rem(mine + k, count)
            pltpu.make_async_remote_copy(
                src_ref=source(to),
                dst_ref=target,
                send_sem=sems.at[base],
                recv_sem=sems.at[base + 1],
                device_id=device(to),
                device_id_type=pl.DeviceIdType.MESH,
            ).start()

        return own

    def finish(own, way, sent, landed, base):
        own.wait()
        whole(sent, way[1] - 1, sems.at[base])
        whole(landed, way[1] - 1, sems.at[base + 1])

    owns = [
        begin(ways[0], lambda to: leaving_ref.at[t, to], middle_ref.at[t, z], 3 * t)
        for t in range(FRONTS)
    ]
    for t in range(FRONTS):
        col = cells_ref[t, 1:2, :]
        hot = (lax.broadcasted_iota(jnp.int32, (SG, VIS), 0) == col).astype(jnp.float32)
        hot = hot.astype(jnp.bfloat16)
        phase_ref[t] = jnp.dot(
            table_ref[0], hot, preferred_element_type=jnp.float32
        ) + jnp.dot(table_ref[1], hot, preferred_element_type=jnp.float32)
    seconds = []
    for t in range(FRONTS):
        finish(owns[t], ways[0], leaving_ref.at[t], middle_ref.at[t], 3 * t)
        seconds.append(
            begin(ways[1], lambda to: middle_ref.at[t, :, to], arrived_ref.at[t, w], 6 + 3 * t)
        )
    scale = SG ** (-0.5)
    returns = []
    for t in range(FRONTS):
        finish(seconds[t], ways[1], middle_ref.at[t], arrived_ref.at[t], 6 + 3 * t)
        row = cells_ref[t, 0:1, :]
        place = lax.broadcasted_iota(jnp.int32, (COLS * groups, VIS), 0)
        hot = (place == row).astype(jnp.float32).astype(jnp.bfloat16)
        turned = (row & 7) * groups + (row >> 3)
        hot_back = (place == turned).astype(jnp.float32).astype(jnp.bfloat16)
        er = phase_ref[t, 0:half, :]
        ei = phase_ref[t, half : 2 * half, :]
        pred_re = jnp.zeros((1, VIS), jnp.float32)
        pred_im = jnp.zeros((1, VIS), jnp.float32)
        for i in range(FACET_ROWS):
            slab = jnp.concatenate(
                [
                    arrived_ref[(t,) + split_index(FACET_ROWS * j + i, deep)].astype(jnp.float32)
                    for j in range(groups)
                ],
                axis=0,
            ).astype(jnp.bfloat16)
            picked = lax.dot_general(
                slab, hot, (((0,), (0,)), ((), ())), preferred_element_type=jnp.float32
            )
            pr = picked[:half]
            pi = picked[half:]
            sr = jnp.sum(pr * er - pi * ei, axis=0, keepdims=True)
            si = jnp.sum(pr * ei + pi * er, axis=0, keepdims=True)
            c8 = phase_ref[t, 2 * half + i : 2 * half + i + 1, :]
            s8 = phase_ref[t, 2 * half + 8 + i : 2 * half + 9 + i, :]
            pred_re += c8 * sr - s8 * si
            pred_im += c8 * si + s8 * sr
        factor = weights_ref[t] * flags_ref[t].astype(jnp.float32)
        res_re = factor * (values_ref[t, 0:1, :] - scale * pred_re) * scale
        res_im = factor * (values_ref[t, 1:2, :] - scale * pred_im) * scale
        for i in range(FACET_ROWS):
            c8 = phase_ref[t, 2 * half + i : 2 * half + i + 1, :]
            s8 = phase_ref[t, 2 * half + 8 + i : 2 * half + 9 + i, :]
            gr = res_re * c8 + res_im * s8
            gi = res_im * c8 - res_re * s8
            wave = jnp.concatenate([gr * er + gi * ei, gi * er - gr * ei], axis=0)
            back = lax.dot_general(
                hot_back,
                wave.astype(jnp.bfloat16),
                (((1,), (1,)), ((), ())),
                preferred_element_type=jnp.float32,
            )
            back_ref[t, :, groups * i : groups * (i + 1), :] = back.reshape(
                COLS, groups, 2 * half
            ).astype(jnp.bfloat16)

        returns.append(
            begin(
                ways[2], lambda to: back_ref.at[t, to], banded_ref.at[t, band], 12 + 3 * t
            )
        )

    for t in range(FRONTS):
        finish(returns[t], ways[2], back_ref.at[t], banded_ref.at[t], 12 + 3 * t)
        total = banded_ref[t, 0].astype(jnp.float32)
        for b in range(1, bands):
            total += banded_ref[t, b].astype(jnp.float32)
        for f in range(facets):
            slot = f % FACET_ROWS * groups + f // FACET_ROWS
            across, along = split_index(f, deep)
            sum_ref[along, across, t : t + 1, :] = total[slot : slot + 1]

    own = begin(ways[0], lambda to: sum_ref.at[to], passing_ref.at[z], 18)
    finish(own, ways[0], sum_ref, passing_ref, 18)
    own = begin(ways[1], lambda to: passing_ref.at[:, to], landed_ref.at[w], 21)
    finish(own, ways[1], passing_ref, landed_ref, 21)

    for t in range(FRONTS):
        for f in range(facets):
            across, along = split_index(f, deep)
            placed_ref[facets * t + f : facets * t + f + 1, :] = landed_ref[
                across, along, t : t + 1, :
            ]
    delivered = placed_ref[...]
    aligned = delivered * ramp_c - swapped(delivered) * ramp_s
    partial = exact_dot(aligned, tables_ref[2])
    first_row = (
        jnp.concatenate([offsets_ref[t : t + 1, :] for t in range(FRONTS)], axis=1) >> 6
    )
    block_row = lax.broadcasted_iota(jnp.int32, (blocks, windows), 0)
    here = (block_row == first_row).astype(jnp.float32)
    after = (block_row == ((first_row + 1) & (blocks - 1))).astype(jnp.float32)
    spread = exact_dot(here, jnp.where(inside, partial, 0.0)) + exact_dot(
        after, jnp.where(inside, 0.0, partial)
    )
    both = exact_dot(tables_ref[3][:, :blocks], spread)
    crossed = swapped(both[half:])
    left_half = left_half[:half]
    line = both[:half] + jnp.where(left_half, -crossed, crossed)
    line = line * tc2 + swapped(line) * jnp.where(left_half, -ts2, ts2)
    ends = exact_dot(tables_ref[4], line, 1, 1)
    ends = jnp.concatenate([ends[:half], ends[half:]], axis=1) * window_ref[...]
    for r in range(2):
        for a in range(chunks):
            out_ref[r : r + 1, 128 * a : 128 * (a + 1)] = ends[
                chunks * r + a : chunks * r + a + 1
            ]


def local(facet_strips, subgrid_offsets, sample_cells, sample_values, sample_weights, sample_flags):
    vmem = pl.BlockSpec(memory_space=pltpu.VMEM)
    facets = lax.axis_size("facet")
    bands = lax.axis_size("band")
    wide = facets // DEEP
    n = np.arange(FN)
    window = (1.0 + 0.5 * np.cos(2.0 * np.pi * n / FN)) * FN ** (-0.5)
    window = np.tile(window.reshape(FN // 128, 128), (2, 1))
    minus = real_form(*unit_table(CONTRIB, -1.0, CONTRIB, CONTRIB))
    plus = real_form(*unit_table(CONTRIB, 1.0, CONTRIB, CONTRIB))
    short = CONTRIB ** (-0.5)
    cosine, sine = unit_table(CONTRIB, 1.0, CONTRIB, CONTRIB)
    stacked = np.zeros((128, 128))
    stacked[:64, :64] = cosine
    stacked[64:, :64] = sine
    ends = plus.T.reshape(2, CONTRIB, 128)
    ordered = np.concatenate([ends[:, 0::2].reshape(64, 128), ends[:, 1::2].reshape(64, 128)])
    tables = np.stack([minus.T, plus * short, minus * short, stacked, ordered])
    split = np.concatenate([minus.T[:, 0::2], minus.T[:, 1::2]], axis=0)
    turn = np.stack([np.tile(x, (1, 2)) for x in unit_table(FN, 1.0, CONTRIB, CONTRIB)])
    lines = pl.pallas_call(
        major_kernel,
        out_shape=jax.ShapeDtypeStruct((2, FN), jnp.float32),
        in_specs=[vmem] * 11,
        out_specs=vmem,
        scratch_shapes=[
            pltpu.VMEM((2 * FN // 128, COLS, 128), jnp.float32),
            pltpu.VMEM((FRONTS, facets, COLS, 128), jnp.float32),
            pltpu.VMEM((FRONTS, DEEP, wide, COLS, 128), jnp.bfloat16),
            pltpu.VMEM((FRONTS, DEEP, wide, COLS, 128), jnp.bfloat16),
            pltpu.VMEM((FRONTS, wide, DEEP, COLS, 128), jnp.bfloat16),
            pltpu.VMEM((FRONTS, 144, VIS), jnp.float32),
            pltpu.VMEM((FRONTS, bands, facets, 128), jnp.bfloat16),
            pltpu.VMEM((FRONTS, bands, facets, 128), jnp.bfloat16),
            pltpu.VMEM((DEEP, wide, FRONTS, 128), jnp.float32),
            pltpu.VMEM((DEEP, wide, FRONTS, 128), jnp.float32),
            pltpu.VMEM((wide, DEEP, FRONTS, 128), jnp.float32),
            pltpu.VMEM((FRONTS * facets, 128), jnp.float32),
            pltpu.SemaphoreType.DMA((24,)),
        ],
        compiler_params=pltpu.CompilerParams(collective_id=0, has_side_effects=True),
    )(
        facet_strips.reshape(2, COLS, FN),
        subgrid_offsets,
        f32(tables),
        f32(split),
        f32(turn),
        f32(window),
        phase_table(),
        sample_cells.reshape(FRONTS, 2, VIS),
        sample_values.reshape(FRONTS, 2, VIS),
        sample_weights.reshape(FRONTS, 1, VIS),
        sample_flags.reshape(FRONTS, 1, VIS),
    )
    return lines.reshape(1, 1, 2, FN)


def solution(mesh):
    placed = (
        P("band", "facet", None, None, None),
        P(),
        P("band", None, "facet", None, None),
        P("band", None, "facet", None, None),
        P("band", None, "facet", None),
        P("band", None, "facet", None),
    )
    return jax.shard_map(
        local, mesh=mesh, in_specs=placed, out_specs=P("facet", "band", None, None), check_vma=False
    )
```

```python
import math

import jax
import jax.numpy as jnp
import numpy as np
from jax import lax
from jax.experimental import pallas as pl
from jax.experimental.pallas import tpu as pltpu
from jax.sharding import PartitionSpec as P

FN = 4096
CONTRIB = 64
FACET_ROWS = 8
COLS = 8
FRONTS = 2
SG = 512
VIS = 512
ROW = 4
DEEP = 8
EXACT = lax.Precision.HIGHEST


def unit_table(length, rotation, rows, cols):
    angle = np.outer(np.arange(rows), np.arange(cols)) % length * (2.0 * np.pi / length)
    return np.cos(angle), rotation * np.sin(angle)


def real_form(cosine, sine):
    return np.block([[cosine, sine], [-sine, cosine]])


def f32(x):
    return jnp.asarray(np.asarray(x, np.float32))


def phase_table():
    cosine, sine = unit_table(SG, -1.0, CONTRIB, SG)
    cos8, sin8 = unit_table(8, -1.0, 8, SG)
    table = np.concatenate([cosine, sine, cos8, sin8], axis=0).astype(np.float32)
    high = table.astype(jnp.bfloat16)
    low = (table - high.astype(np.float32)).astype(jnp.bfloat16)
    return jnp.asarray(np.stack([high, low]))


def swapped(x):
    return jnp.concatenate([x[:, CONTRIB:], x[:, :CONTRIB]], axis=1)


def exact_dot(left, right, left_dim=1, right_dim=0):
    return lax.dot_general(
        left,
        right,
        (((left_dim,), (right_dim,)), ((), ())),
        precision=EXACT,
        preferred_element_type=jnp.float32,
    )


def major_kernel(
    strips_ref,
    offsets_ref,
    tables_ref,
    split_ref,
    turn_ref,
    window_ref,
    table_ref,
    cells_ref,
    values_ref,
    weights_ref,
    flags_ref,
    out_ref,
    strip_ref,
    staged_ref,
    leaving_ref,
    arrived_ref,
    phase_ref,
    back_ref,
    banded_ref,
    sum_ref,
    landed_ref,
    sems,
    ready,
):
    facets = leaving_ref.shape[1]
    bands = back_ref.shape[1]
    groups = facets // FACET_ROWS
    windows = facets * FRONTS
    half = CONTRIB
    blocks = FN // CONTRIB
    me = lax.axis_index("facet")
    band = lax.axis_index("band")
    wide = facets // DEEP
    z = lax.rem(me // ROW, DEEP)
    w = me // (ROW * DEEP) * ROW + lax.rem(me, ROW)

    def along_z(to):
        return {"facet": (w // ROW * DEEP + to) * ROW + lax.rem(w, ROW)}

    def along_w(to):
        return {"facet": (to // ROW * DEEP + z) * ROW + lax.rem(to, ROW)}

    def along_band(to):
        return {"band": to}

    def greet(semaphore, mine, count, device):
        @pl.loop(1, count)
        def _(k):
            pl.semaphore_signal(
                semaphore, inc=1, device_id=device(lax.rem(mine + k, count)),
                device_id_type=pl.DeviceIdType.MESH,
            )


    barrier = pltpu.get_barrier_semaphore()

    greet(barrier, w, wide, along_w)
    greet(barrier, z, DEEP, along_z)
    greet(barrier, band, bands, along_band)

    line_index = lax.broadcasted_iota(jnp.int32, (facets, facets), 0)
    diagonal = line_index == lax.broadcasted_iota(jnp.int32, (facets, facets), 1)
    offsets = jnp.concatenate(
        [
            jnp.sum(jnp.where(diagonal, offsets_ref[t : t + 1, :], 0), axis=1, keepdims=True)
            for t in range(FRONTS)
        ],
        axis=0,
    )
    first = offsets >> 6
    shift = offsets & (half - 1)
    lane = lax.broadcasted_iota(jnp.int32, (windows, 2 * half), 1) & (half - 1)
    inside = lane >= shift
    angle = ((shift * lane) & (half - 1)).astype(jnp.float32) * (2.0 * math.pi / half)
    ramp_c = jnp.cos(angle)
    ramp_s = jnp.sin(angle)
    left_half = lax.broadcasted_iota(jnp.int32, (windows, 2 * half), 1) < half
    ramp_s = jnp.where(left_half, ramp_s, -ramp_s)
    block = lax.broadcasted_iota(jnp.int32, (windows, blocks), 1)
    pick = jnp.concatenate(
        [
            (block == first).astype(jnp.float32),
            (block == ((first + 1) & (blocks - 1))).astype(jnp.float32),
        ],
        axis=0,
    )
    chunks = FN // 128
    for r in range(2):
        for a in range(chunks):
            strip_ref[chunks * r + a] = strips_ref[r, :, 128 * a : 128 * (a + 1)]
    tc2 = turn_ref[0]
    ts2 = turn_ref[1]
    tc = tc2[:, :half]
    ts = ts2[:, :half]
    for c in range(COLS):
        if c == COLS // 2:
            pl.semaphore_wait(barrier, wide + DEEP + bands - 3)
            greet(ready, z, DEEP, along_z)
        section = exact_dot(split_ref[...], strip_ref[:, c, :] * window_ref[...])
        section = section[:128] + swapped(section[128:])
        section = section[:, :half]
        pair = jnp.concatenate(
            [
                section[:half] * tc + section[half:] * ts,
                section[half:] * tc - section[:half] * ts,
            ],
            axis=1,
        )
        spec = exact_dot(tables_ref[0], pair, 1, 1)
        spec = jnp.concatenate([spec[:half], spec[half:]], axis=1)
        chosen = exact_dot(pick, spec)
        cut = jnp.where(inside, chosen[:windows], chosen[windows:])
        piece = exact_dot(cut, tables_ref[1])
        piece = piece * ramp_c + swapped(piece) * ramp_s
        for t in range(FRONTS):
            staged_ref[t, :, c, :] = piece[facets * t : facets * (t + 1)]
    leaving_ref[...] = staged_ref[...].astype(jnp.bfloat16)

    pl.semaphore_wait(ready, DEEP - 1)

    def whole(ref, count, sem):
        part = ref.at[pl.ds(0, count)]
        pltpu.make_async_copy(part, part, sem).wait()

    owns = []
    for t in range(FRONTS):
        own = pltpu.make_async_copy(
            leaving_ref.at[t, me], arrived_ref.at[t, me], sems.at[8 + t]
        )
        own.start()
        owns.append(own)

        @pl.loop(1, facets)
        def _(k):
            to = lax.rem(me + 27 * k, facets)
            pltpu.make_async_remote_copy(
                src_ref=leaving_ref.at[t, to],
                dst_ref=arrived_ref.at[t, me],
                send_sem=sems.at[t],
                recv_sem=sems.at[2 + t],
                device_id={"facet": to},
                device_id_type=pl.DeviceIdType.MESH,
            ).start()

    for t in range(FRONTS):
        col = cells_ref[t, 1:2, :]
        hot = (lax.broadcasted_iota(jnp.int32, (SG, VIS), 0) == col).astype(jnp.float32)
        hot = hot.astype(jnp.bfloat16)
        phase_ref[t] = jnp.dot(
            table_ref[0], hot, preferred_element_type=jnp.float32
        ) + jnp.dot(table_ref[1], hot, preferred_element_type=jnp.float32)
    scale = SG ** (-0.5)
    returns = []
    for t in range(FRONTS):
        owns[t].wait()
        whole(leaving_ref.at[t], facets - 1, sems.at[t])
        whole(arrived_ref.at[t], facets - 1, sems.at[2 + t])
        row = cells_ref[t, 0:1, :]
        place = lax.broadcasted_iota(jnp.int32, (COLS * groups, VIS), 0)
        hot = (place == row).astype(jnp.float32).astype(jnp.bfloat16)
        turned = (row & 7) * groups + (row >> 3)
        hot_back = (place == turned).astype(jnp.float32).astype(jnp.bfloat16)
        er = phase_ref[t, 0:half, :]
        ei = phase_ref[t, half : 2 * half, :]
        pred_re = jnp.zeros((1, VIS), jnp.float32)
        pred_im = jnp.zeros((1, VIS), jnp.float32)
        for i in range(FACET_ROWS):
            slab = jnp.concatenate(
                [
                    arrived_ref[t, FACET_ROWS * j + i].astype(jnp.float32)
                    for j in range(groups)
                ],
                axis=0,
            ).astype(jnp.bfloat16)
            picked = lax.dot_general(
                slab, hot, (((0,), (0,)), ((), ())), preferred_element_type=jnp.float32
            )
            pr = picked[:half]
            pi = picked[half:]
            sr = jnp.sum(pr * er - pi * ei, axis=0, keepdims=True)
            si = jnp.sum(pr * ei + pi * er, axis=0, keepdims=True)
            c8 = phase_ref[t, 2 * half + i : 2 * half + i + 1, :]
            s8 = phase_ref[t, 2 * half + 8 + i : 2 * half + 9 + i, :]
            pred_re += c8 * sr - s8 * si
            pred_im += c8 * si + s8 * sr
        factor = weights_ref[t] * flags_ref[t].astype(jnp.float32)
        res_re = factor * (values_ref[t, 0:1, :] - scale * pred_re) * scale
        res_im = factor * (values_ref[t, 1:2, :] - scale * pred_im) * scale
        for i in range(FACET_ROWS):
            c8 = phase_ref[t, 2 * half + i : 2 * half + i + 1, :]
            s8 = phase_ref[t, 2 * half + 8 + i : 2 * half + 9 + i, :]
            gr = res_re * c8 + res_im * s8
            gi = res_im * c8 - res_re * s8
            wave = jnp.concatenate([gr * er + gi * ei, gi * er - gr * ei], axis=0)
            back = lax.dot_general(
                hot_back,
                wave.astype(jnp.bfloat16),
                (((1,), (1,)), ((), ())),
                preferred_element_type=jnp.float32,
            )
            back_ref[t, :, groups * i : groups * (i + 1), :] = back.reshape(
                COLS, groups, 2 * half
            ).astype(jnp.bfloat16)

        own = pltpu.make_async_copy(
            back_ref.at[t, band], banded_ref.at[t, band], sems.at[10 + t]
        )
        own.start()
        returns.append(own)

        @pl.loop(1, bands)
        def _(k):
            to = lax.rem(band + k, bands)
            pltpu.make_async_remote_copy(
                src_ref=back_ref.at[t, to],
                dst_ref=banded_ref.at[t, band],
                send_sem=sems.at[4 + t],
                recv_sem=sems.at[6 + t],
                device_id={"band": to},
                device_id_type=pl.DeviceIdType.MESH,
            ).start()

    for t in range(FRONTS):
        returns[t].wait()
        whole(back_ref.at[t], bands - 1, sems.at[4 + t])
        whole(banded_ref.at[t], bands - 1, sems.at[6 + t])
        total = banded_ref[t, 0].astype(jnp.float32)
        for b in range(1, bands):
            total += banded_ref[t, b].astype(jnp.float32)
        sum_ref[:, t, :] = total

    mine = lax.rem(me, FACET_ROWS) * groups + me // FACET_ROWS
    own = pltpu.make_async_copy(sum_ref.at[mine], landed_ref.at[me], sems.at[14])
    own.start()

    @pl.loop(1, facets)
    def _(k):
        to = lax.rem(me + 27 * k, facets)
        slot = lax.rem(to, FACET_ROWS) * groups + to // FACET_ROWS
        pltpu.make_async_remote_copy(
            src_ref=sum_ref.at[slot],
            dst_ref=landed_ref.at[me],
            send_sem=sems.at[12],
            recv_sem=sems.at[13],
            device_id={"facet": to},
            device_id_type=pl.DeviceIdType.MESH,
        ).start()

    own.wait()
    whole(sum_ref, facets - 1, sems.at[12])
    whole(landed_ref, facets - 1, sems.at[13])

    delivered = jnp.concatenate([landed_ref[:, t, :] for t in range(FRONTS)], axis=0)
    aligned = delivered * ramp_c - swapped(delivered) * ramp_s
    partial = exact_dot(aligned, tables_ref[2])
    first_row = (
        jnp.concatenate([offsets_ref[t : t + 1, :] for t in range(FRONTS)], axis=1) >> 6
    )
    block_row = lax.broadcasted_iota(jnp.int32, (blocks, windows), 0)
    here = (block_row == first_row).astype(jnp.float32)
    after = (block_row == ((first_row + 1) & (blocks - 1))).astype(jnp.float32)
    spread = exact_dot(here, jnp.where(inside, partial, 0.0)) + exact_dot(
        after, jnp.where(inside, 0.0, partial)
    )
    both = exact_dot(tables_ref[3][:, :blocks], spread)
    crossed = swapped(both[half:])
    left_half = left_half[:half]
    line = both[:half] + jnp.where(left_half, -crossed, crossed)
    line = line * tc2 + swapped(line) * jnp.where(left_half, -ts2, ts2)
    ends = exact_dot(tables_ref[4], line, 1, 1)
    ends = jnp.concatenate([ends[:half], ends[half:]], axis=1) * window_ref[...]
    for r in range(2):
        for a in range(chunks):
            out_ref[r : r + 1, 128 * a : 128 * (a + 1)] = ends[
                chunks * r + a : chunks * r + a + 1
            ]


def local(facet_strips, subgrid_offsets, sample_cells, sample_values, sample_weights, sample_flags):
    vmem = pl.BlockSpec(memory_space=pltpu.VMEM)
    facets = lax.axis_size("facet")
    bands = lax.axis_size("band")
    n = np.arange(FN)
    window = (1.0 + 0.5 * np.cos(2.0 * np.pi * n / FN)) * FN ** (-0.5)
    window = np.tile(window.reshape(FN // 128, 128), (2, 1))
    minus = real_form(*unit_table(CONTRIB, -1.0, CONTRIB, CONTRIB))
    plus = real_form(*unit_table(CONTRIB, 1.0, CONTRIB, CONTRIB))
    short = CONTRIB ** (-0.5)
    cosine, sine = unit_table(CONTRIB, 1.0, CONTRIB, CONTRIB)
    stacked = np.zeros((128, 128))
    stacked[:64, :64] = cosine
    stacked[64:, :64] = sine
    ends = plus.T.reshape(2, CONTRIB, 128)
    ordered = np.concatenate([ends[:, 0::2].reshape(64, 128), ends[:, 1::2].reshape(64, 128)])
    tables = np.stack([minus.T, plus * short, minus * short, stacked, ordered])
    split = np.concatenate([minus.T[:, 0::2], minus.T[:, 1::2]], axis=0)
    turn = np.stack([np.tile(x, (1, 2)) for x in unit_table(FN, 1.0, CONTRIB, CONTRIB)])
    lines = pl.pallas_call(
        major_kernel,
        out_shape=jax.ShapeDtypeStruct((2, FN), jnp.float32),
        in_specs=[vmem] * 11,
        out_specs=vmem,
        scratch_shapes=[
            pltpu.VMEM((2 * FN // 128, COLS, 128), jnp.float32),
            pltpu.VMEM((FRONTS, facets, COLS, 128), jnp.float32),
            pltpu.VMEM((FRONTS, facets, COLS, 128), jnp.bfloat16),
            pltpu.VMEM((FRONTS, facets, COLS, 128), jnp.bfloat16),
            pltpu.VMEM((FRONTS, 144, VIS), jnp.float32),
            pltpu.VMEM((FRONTS, bands, facets, 128), jnp.bfloat16),
            pltpu.VMEM((FRONTS, bands, facets, 128), jnp.bfloat16),
            pltpu.VMEM((facets, FRONTS, 128), jnp.float32),
            pltpu.VMEM((facets, FRONTS, 128), jnp.float32),
            pltpu.SemaphoreType.DMA((15,)),
            pltpu.SemaphoreType.REGULAR,
        ],
        compiler_params=pltpu.CompilerParams(collective_id=0, has_side_effects=True),
    )(
        facet_strips.reshape(2, COLS, FN),
        subgrid_offsets,
        f32(tables),
        f32(split),
        f32(turn),
        f32(window),
        phase_table(),
        sample_cells.reshape(FRONTS, 2, VIS),
        sample_values.reshape(FRONTS, 2, VIS),
        sample_weights.reshape(FRONTS, 1, VIS),
        sample_flags.reshape(FRONTS, 1, VIS),
    )
    return lines.reshape(1, 1, 2, FN)


def solution(mesh):
    placed = (
        P("band", "facet", None, None, None),
        P(),
        P("band", None, "facet", None, None),
        P("band", None, "facet", None, None),
        P("band", None, "facet", None),
        P("band", None, "facet", None),
    )
    return jax.shard_map(
        local, mesh=mesh, in_specs=placed, out_specs=P("facet", "band", None, None), check_vma=False
    )
```

```python
import math

import jax
import jax.numpy as jnp
import numpy as np
from jax import lax
from jax.experimental import pallas as pl
from jax.experimental.pallas import tpu as pltpu
from jax.sharding import PartitionSpec as P

FN = 4096
CONTRIB = 64
FACET_ROWS = 8
COLS = 8
FRONTS = 2
SG = 512
VIS = 512
ROW = 4
DEEP = 8
EXACT = lax.Precision.HIGHEST


def unit_table(length, rotation, rows, cols):
    angle = np.outer(np.arange(rows), np.arange(cols)) % length * (2.0 * np.pi / length)
    return np.cos(angle), rotation * np.sin(angle)


def real_form(cosine, sine):
    return np.block([[cosine, sine], [-sine, cosine]])


def f32(x):
    return jnp.asarray(np.asarray(x, np.float32))


def phase_table():
    cosine, sine = unit_table(SG, -1.0, CONTRIB, SG)
    cos8, sin8 = unit_table(8, -1.0, 8, SG)
    table = np.concatenate([cosine, sine, cos8, sin8], axis=0).astype(np.float32)
    high = table.astype(jnp.bfloat16)
    low = (table - high.astype(np.float32)).astype(jnp.bfloat16)
    return jnp.asarray(np.stack([high, low]))


def swapped(x):
    return jnp.concatenate([x[:, CONTRIB:], x[:, :CONTRIB]], axis=1)


def exact_dot(left, right, left_dim=1, right_dim=0):
    return lax.dot_general(
        left,
        right,
        (((left_dim,), (right_dim,)), ((), ())),
        precision=EXACT,
        preferred_element_type=jnp.float32,
    )


def major_kernel(
    strips_ref,
    offsets_ref,
    tables_ref,
    split_ref,
    turn_ref,
    window_ref,
    table_ref,
    cells_ref,
    values_ref,
    weights_ref,
    flags_ref,
    out_ref,
    strip_ref,
    staged_ref,
    leaving_ref,
    arrived_ref,
    phase_ref,
    back_ref,
    banded_ref,
    sum_ref,
    landed_ref,
    sems,
    ready,
):
    facets = leaving_ref.shape[1]
    bands = back_ref.shape[1]
    groups = facets // FACET_ROWS
    windows = facets * FRONTS
    half = CONTRIB
    blocks = FN // CONTRIB
    me = lax.axis_index("facet")
    band = lax.axis_index("band")
    wide = facets // DEEP
    z = lax.rem(me // ROW, DEEP)
    w = me // (ROW * DEEP) * ROW + lax.rem(me, ROW)

    def along_z(to):
        return {"facet": (w // ROW * DEEP + to) * ROW + lax.rem(w, ROW)}

    def along_w(to):
        return {"facet": (to // ROW * DEEP + z) * ROW + lax.rem(to, ROW)}

    def along_band(to):
        return {"band": to}

    def greet(semaphore, mine, count, device):
        @pl.loop(1, count)
        def _(k):
            pl.semaphore_signal(
                semaphore, inc=1, device_id=device(lax.rem(mine + k, count)),
                device_id_type=pl.DeviceIdType.MESH,
            )


    barrier = pltpu.get_barrier_semaphore()

    greet(barrier, w, wide, along_w)
    greet(barrier, z, DEEP, along_z)
    greet(barrier, band, bands, along_band)

    line_index = lax.broadcasted_iota(jnp.int32, (facets, facets), 0)
    diagonal = line_index == lax.broadcasted_iota(jnp.int32, (facets, facets), 1)
    offsets = jnp.concatenate(
        [
            jnp.sum(jnp.where(diagonal, offsets_ref[t : t + 1, :], 0), axis=1, keepdims=True)
            for t in range(FRONTS)
        ],
        axis=0,
    )
    first = offsets >> 6
    shift = offsets & (half - 1)
    lane = lax.broadcasted_iota(jnp.int32, (windows, 2 * half), 1) & (half - 1)
    inside = lane >= shift
    angle = ((shift * lane) & (half - 1)).astype(jnp.float32) * (2.0 * math.pi / half)
    ramp_c = jnp.cos(angle)
    ramp_s = jnp.sin(angle)
    left_half = lax.broadcasted_iota(jnp.int32, (windows, 2 * half), 1) < half
    ramp_s = jnp.where(left_half, ramp_s, -ramp_s)
    block = lax.broadcasted_iota(jnp.int32, (windows, blocks), 1)
    pick = jnp.concatenate(
        [
            (block == first).astype(jnp.float32),
            (block == ((first + 1) & (blocks - 1))).astype(jnp.float32),
        ],
        axis=0,
    )
    chunks = FN // 128
    for r in range(2):
        for a in range(chunks):
            strip_ref[chunks * r + a] = strips_ref[r, :, 128 * a : 128 * (a + 1)]
    tc2 = turn_ref[0]
    ts2 = turn_ref[1]
    tc = tc2[:, :half]
    ts = ts2[:, :half]
    for c in range(COLS):
        if c == COLS // 2:
            pl.semaphore_wait(barrier, wide + DEEP + bands - 3)
            greet(ready, z, DEEP, along_z)
        section = exact_dot(split_ref[...], strip_ref[:, c, :] * window_ref[...])
        section = section[:128] + swapped(section[128:])
        section = section[:, :half]
        pair = jnp.concatenate(
            [
                section[:half] * tc + section[half:] * ts,
                section[half:] * tc - section[:half] * ts,
            ],
            axis=1,
        )
        spec = exact_dot(tables_ref[0], pair, 1, 1)
        spec = jnp.concatenate([spec[:half], spec[half:]], axis=1)
        chosen = exact_dot(pick, spec)
        cut = jnp.where(inside, chosen[:windows], chosen[windows:])
        piece = exact_dot(cut, tables_ref[1])
        piece = piece * ramp_c + swapped(piece) * ramp_s
        for t in range(FRONTS):
            staged_ref[t, :, c, :] = piece[facets * t : facets * (t + 1)]
    leaving_ref[...] = staged_ref[...].astype(jnp.bfloat16)

    pl.semaphore_wait(ready, DEEP - 1)

    def whole(ref, count, sem):
        part = ref.at[pl.ds(0, count)]
        pltpu.make_async_copy(part, part, sem).wait()

    far = facets // 2

    def send(t, to):
        pltpu.make_async_remote_copy(
            src_ref=leaving_ref.at[t, to],
            dst_ref=arrived_ref.at[t, me],
            send_sem=sems.at[t],
            recv_sem=sems.at[2 + t],
            device_id={"facet": to},
            device_id_type=pl.DeviceIdType.MESH,
        ).start()

    owns = []
    for t in range(FRONTS):
        own = pltpu.make_async_copy(
            leaving_ref.at[t, me], arrived_ref.at[t, me], sems.at[8 + t]
        )
        own.start()
        owns.append(own)

        @pl.loop(0, far)
        def _(k):
            send(t, lax.rem(me // far + 1, 2) * far + lax.rem(me + 11 * k, far))

        @pl.loop(1, far)
        def _(k):
            send(t, me // far * far + lax.rem(me + 11 * k, far))

    for t in range(FRONTS):
        col = cells_ref[t, 1:2, :]
        hot = (lax.broadcasted_iota(jnp.int32, (SG, VIS), 0) == col).astype(jnp.float32)
        hot = hot.astype(jnp.bfloat16)
        phase_ref[t] = jnp.dot(
            table_ref[0], hot, preferred_element_type=jnp.float32
        ) + jnp.dot(table_ref[1], hot, preferred_element_type=jnp.float32)
    scale = SG ** (-0.5)
    returns = []
    for t in range(FRONTS):
        owns[t].wait()
        whole(leaving_ref.at[t], facets - 1, sems.at[t])
        whole(arrived_ref.at[t], facets - 1, sems.at[2 + t])
        row = cells_ref[t, 0:1, :]
        place = lax.broadcasted_iota(jnp.int32, (COLS * groups, VIS), 0)
        hot = (place == row).astype(jnp.float32).astype(jnp.bfloat16)
        turned = (row & 7) * groups + (row >> 3)
        hot_back = (place == turned).astype(jnp.float32).astype(jnp.bfloat16)
        er = phase_ref[t, 0:half, :]
        ei = phase_ref[t, half : 2 * half, :]
        pred_re = jnp.zeros((1, VIS), jnp.float32)
        pred_im = jnp.zeros((1, VIS), jnp.float32)
        for i in range(FACET_ROWS):
            slab = jnp.concatenate(
                [
                    arrived_ref[t, FACET_ROWS * j + i].astype(jnp.float32)
                    for j in range(groups)
                ],
                axis=0,
            ).astype(jnp.bfloat16)
            picked = lax.dot_general(
                slab, hot, (((0,), (0,)), ((), ())), preferred_element_type=jnp.float32
            )
            pr = picked[:half]
            pi = picked[half:]
            sr = jnp.sum(pr * er - pi * ei, axis=0, keepdims=True)
            si = jnp.sum(pr * ei + pi * er, axis=0, keepdims=True)
            c8 = phase_ref[t, 2 * half + i : 2 * half + i + 1, :]
            s8 = phase_ref[t, 2 * half + 8 + i : 2 * half + 9 + i, :]
            pred_re += c8 * sr - s8 * si
            pred_im += c8 * si + s8 * sr
        factor = weights_ref[t] * flags_ref[t].astype(jnp.float32)
        res_re = factor * (values_ref[t, 0:1, :] - scale * pred_re) * scale
        res_im = factor * (values_ref[t, 1:2, :] - scale * pred_im) * scale
        for i in range(FACET_ROWS):
            c8 = phase_ref[t, 2 * half + i : 2 * half + i + 1, :]
            s8 = phase_ref[t, 2 * half + 8 + i : 2 * half + 9 + i, :]
            gr = res_re * c8 + res_im * s8
            gi = res_im * c8 - res_re * s8
            wave = jnp.concatenate([gr * er + gi * ei, gi * er - gr * ei], axis=0)
            back = lax.dot_general(
                hot_back,
                wave.astype(jnp.bfloat16),
                (((1,), (1,)), ((), ())),
                preferred_element_type=jnp.float32,
            )
            back_ref[t, :, groups * i : groups * (i + 1), :] = back.reshape(
                COLS, groups, 2 * half
            ).astype(jnp.bfloat16)

        own = pltpu.make_async_copy(
            back_ref.at[t, band], banded_ref.at[t, band], sems.at[10 + t]
        )
        own.start()
        returns.append(own)

        @pl.loop(1, bands)
        def _(k):
            to = lax.rem(band + k, bands)
            pltpu.make_async_remote_copy(
                src_ref=back_ref.at[t, to],
                dst_ref=banded_ref.at[t, band],
                send_sem=sems.at[4 + t],
                recv_sem=sems.at[6 + t],
                device_id={"band": to},
                device_id_type=pl.DeviceIdType.MESH,
            ).start()

    for t in range(FRONTS):
        returns[t].wait()
        whole(back_ref.at[t], bands - 1, sems.at[4 + t])
        whole(banded_ref.at[t], bands - 1, sems.at[6 + t])
        total = banded_ref[t, 0].astype(jnp.float32)
        for b in range(1, bands):
            total += banded_ref[t, b].astype(jnp.float32)
        sum_ref[:, t, :] = total

    mine = lax.rem(me, FACET_ROWS) * groups + me // FACET_ROWS
    own = pltpu.make_async_copy(sum_ref.at[mine], landed_ref.at[me], sems.at[14])
    own.start()

    @pl.loop(1, facets)
    def _(k):
        to = lax.rem(me + 27 * k, facets)
        slot = lax.rem(to, FACET_ROWS) * groups + to // FACET_ROWS
        pltpu.make_async_remote_copy(
            src_ref=sum_ref.at[slot],
            dst_ref=landed_ref.at[me],
            send_sem=sems.at[12],
            recv_sem=sems.at[13],
            device_id={"facet": to},
            device_id_type=pl.DeviceIdType.MESH,
        ).start()

    own.wait()
    whole(sum_ref, facets - 1, sems.at[12])
    whole(landed_ref, facets - 1, sems.at[13])

    delivered = jnp.concatenate([landed_ref[:, t, :] for t in range(FRONTS)], axis=0)
    aligned = delivered * ramp_c - swapped(delivered) * ramp_s
    partial = exact_dot(aligned, tables_ref[2])
    first_row = (
        jnp.concatenate([offsets_ref[t : t + 1, :] for t in range(FRONTS)], axis=1) >> 6
    )
    block_row = lax.broadcasted_iota(jnp.int32, (blocks, windows), 0)
    here = (block_row == first_row).astype(jnp.float32)
    after = (block_row == ((first_row + 1) & (blocks - 1))).astype(jnp.float32)
    spread = exact_dot(here, jnp.where(inside, partial, 0.0)) + exact_dot(
        after, jnp.where(inside, 0.0, partial)
    )
    both = exact_dot(tables_ref[3][:, :blocks], spread)
    crossed = swapped(both[half:])
    left_half = left_half[:half]
    line = both[:half] + jnp.where(left_half, -crossed, crossed)
    line = line * tc2 + swapped(line) * jnp.where(left_half, -ts2, ts2)
    ends = exact_dot(tables_ref[4], line, 1, 1)
    ends = jnp.concatenate([ends[:half], ends[half:]], axis=1) * window_ref[...]
    for r in range(2):
        for a in range(chunks):
            out_ref[r : r + 1, 128 * a : 128 * (a + 1)] = ends[
                chunks * r + a : chunks * r + a + 1
            ]


def local(facet_strips, subgrid_offsets, sample_cells, sample_values, sample_weights, sample_flags):
    vmem = pl.BlockSpec(memory_space=pltpu.VMEM)
    facets = lax.axis_size("facet")
    bands = lax.axis_size("band")
    n = np.arange(FN)
    window = (1.0 + 0.5 * np.cos(2.0 * np.pi * n / FN)) * FN ** (-0.5)
    window = np.tile(window.reshape(FN // 128, 128), (2, 1))
    minus = real_form(*unit_table(CONTRIB, -1.0, CONTRIB, CONTRIB))
    plus = real_form(*unit_table(CONTRIB, 1.0, CONTRIB, CONTRIB))
    short = CONTRIB ** (-0.5)
    cosine, sine = unit_table(CONTRIB, 1.0, CONTRIB, CONTRIB)
    stacked = np.zeros((128, 128))
    stacked[:64, :64] = cosine
    stacked[64:, :64] = sine
    ends = plus.T.reshape(2, CONTRIB, 128)
    ordered = np.concatenate([ends[:, 0::2].reshape(64, 128), ends[:, 1::2].reshape(64, 128)])
    tables = np.stack([minus.T, plus * short, minus * short, stacked, ordered])
    split = np.concatenate([minus.T[:, 0::2], minus.T[:, 1::2]], axis=0)
    turn = np.stack([np.tile(x, (1, 2)) for x in unit_table(FN, 1.0, CONTRIB, CONTRIB)])
    lines = pl.pallas_call(
        major_kernel,
        out_shape=jax.ShapeDtypeStruct((2, FN), jnp.float32),
        in_specs=[vmem] * 11,
        out_specs=vmem,
        scratch_shapes=[
            pltpu.VMEM((2 * FN // 128, COLS, 128), jnp.float32),
            pltpu.VMEM((FRONTS, facets, COLS, 128), jnp.float32),
            pltpu.VMEM((FRONTS, facets, COLS, 128), jnp.bfloat16),
            pltpu.VMEM((FRONTS, facets, COLS, 128), jnp.bfloat16),
            pltpu.VMEM((FRONTS, 144, VIS), jnp.float32),
            pltpu.VMEM((FRONTS, bands, facets, 128), jnp.bfloat16),
            pltpu.VMEM((FRONTS, bands, facets, 128), jnp.bfloat16),
            pltpu.VMEM((facets, FRONTS, 128), jnp.float32),
            pltpu.VMEM((facets, FRONTS, 128), jnp.float32),
            pltpu.SemaphoreType.DMA((15,)),
            pltpu.SemaphoreType.REGULAR,
        ],
        compiler_params=pltpu.CompilerParams(collective_id=0, has_side_effects=True),
    )(
        facet_strips.reshape(2, COLS, FN),
        subgrid_offsets,
        f32(tables),
        f32(split),
        f32(turn),
        f32(window),
        phase_table(),
        sample_cells.reshape(FRONTS, 2, VIS),
        sample_values.reshape(FRONTS, 2, VIS),
        sample_weights.reshape(FRONTS, 1, VIS),
        sample_flags.reshape(FRONTS, 1, VIS),
    )
    return lines.reshape(1, 1, 2, FN)


def solution(mesh):
    placed = (
        P("band", "facet", None, None, None),
        P(),
        P("band", None, "facet", None, None),
        P("band", None, "facet", None, None),
        P("band", None, "facet", None),
        P("band", None, "facet", None),
    )
    return jax.shard_map(
        local, mesh=mesh, in_specs=placed, out_specs=P("facet", "band", None, None), check_vma=False
    )
```
